32 devices in a mesh: grp: 4 (over y, x), seq: 8 (over z, core).
Axes of the slice: x: 2, y: 2, z: 4, core: 2. Of those that a mesh axis runs over, the one named last changes fastest.
Arguments:
- queries: bfloat16 [1024, 64, 192], P('seq', 'grp'), may hold values from -6 to 6
- key_cache: bfloat16 [4, 8192, 192], P('grp', 'seq'), may hold values from -6 to 6
- group_value_cache: bfloat16 [4, 8192, 128], P('grp', 'seq'), may hold values from -6 to 6
- coarse_keys: bfloat16 [4, 512, 192], P('grp', 'seq'), may hold values from -6 to 6
- coarse_values: bfloat16 [4, 512, 128], P('grp', 'seq'), may hold values from -6 to 6
- hidden: bfloat16 [1024, 2560], P('seq'), may hold values from -6 to 6
- gate_weight: bfloat16 [4, 2560, 32], P('grp'), may hold values from -0.125 to 0.125
- out_weight: bfloat16 [8192, 2560], P('grp'), may hold values from -0.09375 to 0.09375
- selected: int32 [4, 8, 16], P('grp', 'seq'), may hold values from 0 to 127, as said below
Outputs:
- layer_out: bfloat16 [1024, 2560], P('seq', 'grp')
The draws below stay inside these ranges and needn't reach their ends.
Inputs may be any that keep to these rules, and one draw needn't show every extreme that they name: selected[g, t] lists 16 distinct blocks of 64 positions for tile t of group g; the first is block 0; none starts after the tile's last query position; at most 4 of them lie within one index of seq's 1024 positions.
All inputs are finite; a program needn't handle non-finite values.
Results may differ from the reference program's by a relative error of at most 0.013.
Values may be sent and summed in bfloat16 or wider, within the bound.
A program may use at most 128 MiB of HBM per device.

```python
import jax
import jax.numpy as jnp
from jax import lax

D = 2560
HEADS = 64
GROUPS = 4
DQK = 192
DV = 128
BLK = 64
SEL = 16
TILE = 128
CSTRIDE = 16
CLEN = 32
HG = 16
TILES = 8
NQ = 1024
CONTEXT = 8192
NC = 512
BLK_DEV = 16
CAP = 4
N_SEQ = 8


def draw_queries(key, part):
    full_shape = (NQ, HEADS, DQK)
    return jnp.clip(jax.random.normal(jax.random.fold_in(key, 11), full_shape, jnp.float32), -6.0, 6.0).astype(jnp.bfloat16)


def draw_key_cache(key, part):
    full_shape = (GROUPS, CONTEXT, DQK)
    return jnp.clip(jax.random.normal(jax.random.fold_in(key, 21), full_shape, jnp.float32), -6.0, 6.0).astype(jnp.bfloat16)


def draw_coarse_keys(key, part):
    full_shape = (GROUPS, NC, DQK)
    return jnp.clip(jax.random.normal(jax.random.fold_in(key, 23), full_shape, jnp.float32), -6.0, 6.0).astype(jnp.bfloat16)


def draw_selected(key, part):
    tile_ids = jnp.arange(TILES, dtype=jnp.int32)
    last_block = (CONTEXT - NQ + (tile_ids + 1) * TILE - 1) // BLK
    last_owner = last_block // BLK_DEV
    owner_ids = jnp.arange(N_SEQ, dtype=jnp.int32)
    slot_ids = jnp.arange(CAP, dtype=jnp.int32)
    owned = jnp.where(owner_ids[None, :] < last_owner[:, None], BLK_DEV, jnp.where(owner_ids[None, :] == last_owner[:, None], last_block[:, None] - last_owner[:, None] * BLK_DEV + 1, 0))
    is_first = (owner_ids[None, :] == 0).astype(jnp.int32)
    usable = owned - is_first
    slot_limit = jnp.minimum(usable, CAP - is_first)
    open_slot = slot_ids[None, None, :] < slot_limit[:, :, None]
    latest_blocks = owner_ids[None, :] >= last_owner[:, None] - 1
    preferred_blocks = (owner_ids[None, :] <= 1) | (owner_ids[None, :] >= last_owner[:, None] - 6)
    preference_boost = jnp.where(latest_blocks, 2 ** 20, 0) + jnp.where(preferred_blocks, 2 ** 16, 0)
    random_noise = jax.random.randint(jax.random.fold_in(key, 31), (GROUPS, TILES, N_SEQ, CAP), 0, 2 ** 16)
    logit_scores = random_noise + preference_boost[None, :, :, None]
    flat_ids = owner_ids[:, None] * CAP + slot_ids[None, :]
    ranked = jnp.where(open_slot[None], logit_scores + 1, 0) * (N_SEQ * CAP) + flat_ids[None, None]
    ranked = ranked.reshape(GROUPS, TILES, N_SEQ * CAP)
    top_values, chosen = lax.top_k(ranked, SEL - 1)
    chosen_owner = chosen // CAP
    chosen_slot = chosen % CAP
    rotation = jax.random.randint(jax.random.fold_in(key, 37), (GROUPS, TILES, N_SEQ), 0, 2 ** 20)
    usable_all = jnp.broadcast_to(usable[None], (GROUPS, TILES, N_SEQ))
    block_span = jnp.maximum(jnp.take_along_axis(usable_all, chosen_owner, axis=2), 1)
    start_pick = jnp.take_along_axis(rotation, chosen_owner, axis=2) % block_span
    within = (start_pick + chosen_slot) % block_span + (chosen_owner == 0).astype(jnp.int32)
    blocks = chosen_owner * BLK_DEV + within
    sink_block = jnp.zeros((GROUPS, TILES, 1), jnp.int32)
    return jnp.concatenate([sink_block, blocks.astype(jnp.int32)], axis=2)


def spiked(drawn, key, source, target, shards_of, factor):
    def block_of(dim):
        return (jnp.arange(drawn.shape[dim]) // (drawn.shape[dim] // shards_of)).reshape((-1,) + (1,) * (drawn.ndim - 1 - dim))

    first = jax.random.permutation(key, shards_of)[block_of(target)]
    far = (block_of(target) + shards_of // 2) % shards_of
    return jnp.where((block_of(source) == first) | (block_of(source) == far), factor * drawn, drawn)


def shard_levels(rng, dims, cuts, smallest, high):
    level = 1.0
    for position, blocks in cuts:
        steps = jax.random.uniform(jax.random.fold_in(jax.random.fold_in(rng, 6), position), (blocks,), jnp.float32, smallest / len(cuts), high / len(cuts))
        level = level * jnp.repeat(jnp.exp(steps), dims[position] // blocks).reshape((-1,) + (1,) * (len(dims) - 1 - position))
    return level


def gaussian(key, shape, scale, most, shards=(), kind=jnp.bfloat16):
    entries = scale * jax.random.normal(key, shape, jnp.float32)
    if shards:
        entries = entries * shard_levels(key, shape, shards, -0.22, 0.18)
    return jnp.clip(entries, -most, most).astype(kind)


def gaussian_with(key, dims, scale, most, split, heavy, kind=jnp.bfloat16):
    drawn = scale * jax.random.normal(key, dims, jnp.float32)
    if split:
        drawn = drawn * shard_levels(key, dims, split, -0.22, 0.18)
    return jnp.clip(spiked(drawn, jax.random.fold_in(key, 3), *heavy), -most, most).astype(kind)


def setup_inputs(seed: int = 0) -> dict:
    streams_of = jax.random.split(jax.random.key(seed), 10)
    return {
        "queries": draw_queries(jax.random.fold_in(streams_of[9], 71), 0),
        "key_cache": draw_key_cache(jax.random.fold_in(streams_of[9], 71), 0),
        "group_value_cache": gaussian(streams_of[2], (GROUPS, CONTEXT, DV), 1.0, 6.0, ((0, 4), (1, 8))),
        "coarse_keys": draw_coarse_keys(jax.random.fold_in(streams_of[9], 71), 0),
        "coarse_values": gaussian(streams_of[4], (GROUPS, NC, DV), 1.0, 6.0, ((0, 4), (1, 8))),
        "hidden": gaussian(streams_of[5], (NQ, D), 1.0, 6.0, ((0, 8),)),
        "gate_weight": gaussian(streams_of[6], (GROUPS, D, 2 * HG), D ** -0.5, 0.125, ((0, 4),)),
        "out_weight": gaussian_with(streams_of[7], (HEADS * DV, D), (HEADS * DV) ** -0.5, 0.09375, ((0, 4),), (0, 1, 4, 2.0)),
        "selected": draw_selected(jax.random.fold_in(streams_of[9], 71), 0),
    }


def branch(query_rows, row_pos, key_rows, value_rows, key_pos):
    logit_scores = jnp.dot(query_rows, key_rows.T, preferred_element_type=jnp.float32) * (DQK ** -0.5)
    logit_scores = jnp.where(key_pos[None, :] <= row_pos[:, None], logit_scores, -jnp.inf)
    row_max = jnp.max(logit_scores, axis=1, keepdims=True)
    weights = jnp.exp(logit_scores - row_max)
    row_total = jnp.sum(weights, axis=1, keepdims=True)
    return jnp.dot(weights.astype(jnp.bfloat16), value_rows, preferred_element_type=jnp.float32) / row_total


def reference(queries, key_cache, group_value_cache, coarse_keys, coarse_values, hidden, gate_weight, out_weight, selected):
    coarse_pos = jnp.arange(NC, dtype=jnp.int32) * CSTRIDE + CLEN - 1
    offsets = jnp.arange(BLK, dtype=jnp.int32)

    def one_tile(flat_index):
        group_index = (flat_index // TILES).astype(jnp.int32)
        tile_index = (flat_index % TILES).astype(jnp.int32)
        first_row = (tile_index * TILE).astype(jnp.int32)
        query_rows = lax.dynamic_slice(queries, (first_row, (group_index * HG).astype(jnp.int32), jnp.int32(0)), (TILE, HG, DQK)).reshape(TILE * HG, DQK)
        query_pos = (CONTEXT - NQ + first_row + jnp.arange(TILE, dtype=jnp.int32)).astype(jnp.int32)
        row_pos = jnp.repeat(query_pos, HG)
        group_keys = lax.dynamic_index_in_dim(key_cache, group_index, 0, keepdims=False)
        group_values = lax.dynamic_index_in_dim(group_value_cache, group_index, 0, keepdims=False)
        coarse_k = lax.dynamic_index_in_dim(coarse_keys, group_index, 0, keepdims=False)
        coarse_v = lax.dynamic_index_in_dim(coarse_values, group_index, 0, keepdims=False)
        coarse = branch(query_rows, row_pos, coarse_k, coarse_v, coarse_pos)
        group_sel = lax.dynamic_index_in_dim(selected, group_index, 0, keepdims=False)
        blocks = lax.dynamic_index_in_dim(group_sel, tile_index, 0, keepdims=False)
        key_pos = (blocks[:, None] * BLK + offsets[None, :]).reshape(-1).astype(jnp.int32)
        picked_block_index = branch(query_rows, row_pos, group_keys[key_pos], group_values[key_pos], key_pos)
        tile_hidden = lax.dynamic_slice_in_dim(hidden, first_row, TILE, 0)
        group_gate = lax.dynamic_index_in_dim(gate_weight, group_index, 0, keepdims=False)
        gate_logits = jnp.dot(tile_hidden, group_gate, preferred_element_type=jnp.float32)
        gate_coarse = jax.nn.sigmoid(gate_logits[:, :HG])
        gate_picked = jax.nn.sigmoid(gate_logits[:, HG:])
        mixed_heads = gate_coarse[:, :, None] * coarse.reshape(TILE, HG, DV) + gate_picked[:, :, None] * picked_block_index.reshape(TILE, HG, DV)
        return mixed_heads.astype(jnp.bfloat16).reshape(TILE, HG * DV)

    tiles_out = lax.map(one_tile, jnp.arange(GROUPS * TILES, dtype=jnp.int32))
    attended = tiles_out.reshape(GROUPS, TILES, TILE, HG * DV).transpose(1, 2, 0, 3).reshape(NQ, HEADS * DV)
    return jnp.dot(attended, out_weight, preferred_element_type=jnp.float32).astype(jnp.bfloat16)
```

```python
import functools
import math

import jax
import jax.numpy as jnp
from jax import lax
from jax.experimental import pallas as pl
from jax.experimental.pallas import tpu as pltpu
from jax.sharding import PartitionSpec as P

BLK = 64
SEL = 16
TILE = 128
CSTRIDE = 16
CLEN = 32

NEGATIVE = -1e30
FAR = 1 << 28
ROWS = 256
MESH = pl.DeviceIdType.MESH
HALF = BLK // 2
UNIT = BLK + HALF + BLK


def pack(keys, values, width):
    tail = keys[:, 128:width]
    folded = jnp.concatenate([tail[:HALF], tail[HALF:]], axis=1)
    return jnp.concatenate([keys[:, :128], folded, values], axis=0)


def unpack(block):
    folded = block[BLK : BLK + HALF]
    low = lax.broadcasted_iota(jnp.int32, folded.shape, 1) < 64
    zero = jnp.zeros_like(folded)
    tails = jnp.concatenate([jnp.where(low, folded, zero), jnp.where(low, zero, folded)], axis=0)
    keys = jnp.concatenate([block[:BLK], tails], axis=1)
    values = block[BLK + HALF :]
    return keys, jnp.concatenate([values, jnp.ones_like(values)], axis=1)


def kernel(
    n,
    groups,
    cap,
    scale,
    table_smem,
    table_ref,
    kpos_ref,
    query_ref,
    key_ref,
    value_ref,
    ckey_ref,
    cvalue_ref,
    hidden_ref,
    gate_ref,
    weight_ref,
    out_ref,
    packed,
    query_wide,
    tables,
    tables_smem,
    outgoing,
    incoming,
    coarse,
    keys_wide,
    values_wide,
    running,
    picked_sum,
    coarse_sum,
    attended,
    weights,
    partial,
    arrived,
    own_part,
    weight_sem,
    local_sem,
    table_send,
    table_recv,
    slot_send,
    slot_recv,
    coarse_send,
    coarse_recv,
    pass_send,
    pass_recv,
    part_send,
    part_recv,
):
    me = lax.axis_index("seq")
    group = lax.axis_index("grp")
    core = lax.rem(me, 2)
    sibling = me + 1 - 2 * core
    rows = query_ref.shape[0]
    width = query_ref.shape[1]
    heads = rows // TILE
    blocks = key_ref.shape[0]
    columns = out_ref.shape[1]
    context = blocks * BLK * n

    def weight_copy(step):
        target = lax.rem(group + step, groups)
        return pltpu.make_async_copy(
            weight_ref.at[:, pl.ds(pl.multiple_of(target * columns, 128), columns)],
            weights.at[step],
            weight_sem.at[step],
        )

    for step in range(groups):
        weight_copy(step).start()

    barrier = pltpu.get_barrier_semaphore()

    def greet(step, carry):
        pl.semaphore_signal(
            barrier, inc=1, device_id={"seq": lax.rem(me + step, n)}, device_id_type=MESH
        )
        return carry

    lax.fori_loop(1, n, greet, 0)
    for step in range(1, groups):
        pl.semaphore_signal(
            barrier, inc=1, device_id={"grp": lax.rem(group + step, groups)}, device_id_type=MESH
        )

    coarse[me] = pack(ckey_ref[...], cvalue_ref[...], width)

    def pack_one(index, carry):
        packed[index] = pack(key_ref[index], value_ref[index], width)
        return carry

    lax.fori_loop(0, blocks, pack_one, 0)
    pl.semaphore_wait(barrier, n - 1 + groups - 1)

    def table_copy(step):
        return pltpu.make_async_remote_copy(
            src_ref=table_ref,
            dst_ref=tables.at[step],
            send_sem=table_send.at[step],
            recv_sem=table_recv.at[step],
            device_id={"seq": lax.rem(me + step, n)},
            device_id_type=MESH,
        )

    def coarse_copy(step):
        return pltpu.make_async_remote_copy(
            src_ref=coarse.at[me],
            dst_ref=coarse.at[me],
            send_sem=coarse_send.at[step],
            recv_sem=coarse_recv.at[step],
            device_id={"seq": lax.rem(me + 2 * step, n)},
            device_id_type=MESH,
        )

    def pass_copy(step):
        origin = lax.rem(me - 2 * step + n, n)
        return pltpu.make_async_remote_copy(
            src_ref=coarse.at[origin],
            dst_ref=coarse.at[origin],
            send_sem=pass_send.at[step],
            recv_sem=pass_recv.at[step],
            device_id={"seq": sibling},
            device_id_type=MESH,
        )

    def slot_copy(step):
        return pltpu.make_async_remote_copy(
            src_ref=outgoing.at[step],
            dst_ref=incoming.at[step],
            send_sem=slot_send.at[step],
            recv_sem=slot_recv.at[step],
            device_id={"seq": lax.rem(me + step, n)},
            device_id_type=MESH,
        )

    def send_table(step, carry):
        table_copy(step).start()
        return carry

    lax.fori_loop(1, n, send_table, 0)

    def send_coarse(step, carry):
        coarse_copy(step).start()
        return carry

    lax.fori_loop(1, n // 2, send_coarse, 0)
    pass_copy(0).start()

    for slot in range(cap):
        incoming[0, slot] = packed[table_smem[0, me * cap + slot]]
    main = query_ref[:, :128]
    tail = query_ref[:, 128:width]
    query_wide[:, :128] = main
    query_wide[:, 128:] = jnp.concatenate([tail, tail], axis=1)

    def wait_table(step, carry):
        table_copy(step).wait_recv()
        return carry

    lax.fori_loop(1, n, wait_table, 0)
    to_smem = pltpu.make_async_copy(tables, tables_smem, local_sem)
    to_smem.start()
    to_smem.wait()

    def send_slots(index, carry):
        step = n // 2 + index
        for slot in range(cap):
            outgoing[step, slot] = packed[tables_smem[n - step, 0, me * cap + slot]]
        slot_copy(step).start()
        return carry

    lax.fori_loop(0, n // 2, send_slots, 0)

    def send_slots_low(index, carry):
        step = n // 2 - 1 - index
        for slot in range(cap):
            outgoing[step, slot] = packed[tables_smem[n - step, 0, me * cap + slot]]
        slot_copy(step).start()
        return carry

    lax.fori_loop(0, n // 2 - 1, send_slots_low, 0)

    first_pos = context - TILE * n + me * TILE

    def attend(kpos, width_keys, total, first):
        relative = kpos - first_pos
        offsets = lax.broadcasted_iota(jnp.int32, (ROWS, width_keys), 0) // heads

        def chunk(index, carry):
            at = pl.multiple_of(index * ROWS, ROWS)
            here = pl.ds(at, ROWS)
            scores = lax.dot_general(
                query_wide[here, :],
                keys_wide[:width_keys],
                (((1,), (1,)), ((), ())),
                preferred_element_type=jnp.float32,
            )
            seen = relative - index * (ROWS // heads) <= offsets
            scores = jnp.where(seen, scores, -jnp.inf)
            top = jnp.max(scores, axis=1, keepdims=True)
            old = jnp.where(first, jnp.full((ROWS, 128), NEGATIVE, jnp.float32), running[here, :])
            new = jnp.maximum(old, top)
            factor = jnp.exp2((old - new) * scale)
            exponents = jnp.exp2((scores - new[:, :1]) * scale).astype(jnp.bfloat16)
            added = jnp.dot(
                exponents, values_wide[:width_keys], preferred_element_type=jnp.float32
            )
            for part in range(2):
                before = total[part, here, :]
                before = jnp.where(first, jnp.zeros_like(before), before)
                total[part, here, :] = before * factor + added[:, part * 128 : part * 128 + 128]
            running[here, :] = new
            return carry

        lax.fori_loop(0, rows // ROWS, chunk, 0)

    gates = jax.nn.sigmoid(
        jnp.dot(hidden_ref[...], gate_ref[...], preferred_element_type=jnp.float32)
    )

    def forward(step, carry):
        coarse_copy(step).wait_recv()
        pass_copy(step).start()
        return carry

    lax.fori_loop(1, n // 2, forward, 0)

    def passed(step, carry):
        pass_copy(step).wait_recv()
        return carry

    lax.fori_loop(0, n // 2, passed, 0)

    pieces = min(n, 8)

    def coarse_step(index, carry):
        for piece in range(pieces):
            keys, values = unpack(coarse[index * pieces + piece])
            keys_wide[piece * BLK : (piece + 1) * BLK] = keys
            values_wide[piece * BLK : (piece + 1) * BLK] = values
        token = lax.broadcasted_iota(jnp.int32, (1, pieces * BLK), 1) + index * (pieces * BLK)
        attend(token * CSTRIDE + CLEN - 1, pieces * BLK, coarse_sum, index == 0)
        return carry

    lax.fori_loop(0, n // pieces, coarse_step, 0)

    def picked_step(step, carry):
        @pl.when(step > 0)
        def _():
            slot_copy(jnp.maximum(step, 1)).wait_recv()

        for slot in range(cap):
            keys, values = unpack(incoming[step, slot])
            keys_wide[slot * BLK : (slot + 1) * BLK] = keys
            values_wide[slot * BLK : (slot + 1) * BLK] = values
        owner = lax.rem(me - step + n, n)
        attend(kpos_ref[owner], cap * BLK, picked_sum, step == 0)
        return carry

    lax.fori_loop(0, n, picked_step, 0)

    for head in range(heads):
        mine = pl.ds(head, TILE, stride=heads)
        of_coarse = coarse_sum[0, mine, :] / coarse_sum[1, mine, :]
        of_picked = picked_sum[0, mine, :] / picked_sum[1, mine, :]
        mixed = gates[:, head : head + 1] * of_coarse + gates[:, heads + head : heads + head + 1] * of_picked
        attended[:, head * 128 : (head + 1) * 128] = mixed.astype(jnp.bfloat16)

    def part_copy(step):
        return pltpu.make_async_remote_copy(
            src_ref=partial.at[step],
            dst_ref=arrived.at[step],
            send_sem=part_send.at[step],
            recv_sem=part_recv.at[step],
            device_id={"grp": lax.rem(group + step, groups)},
            device_id_type=MESH,
        )

    for step in range(1, groups):
        weight_copy(step).wait()
        partial[step] = jnp.dot(
            attended[...], weights[step], preferred_element_type=jnp.float32
        ).astype(jnp.bfloat16)
        part_copy(step).start()
    weight_copy(0).wait()
    own_part[...] = jnp.dot(attended[...], weights[0], preferred_element_type=jnp.float32)

    def sent(step, carry):
        table_copy(step).wait_send()
        slot_copy(step).wait_send()
        return carry

    lax.fori_loop(1, n, sent, 0)

    def sent_coarse(step, carry):
        coarse_copy(step).wait_send()
        pass_copy(step).wait_send()
        return carry

    lax.fori_loop(1, n // 2, sent_coarse, 0)
    pass_copy(0).wait_send()
    total = own_part[...]
    for step in range(1, groups):
        part_copy(step).wait_recv()
        total = total + arrived[step].astype(jnp.float32)
    out_ref[...] = total.astype(out_ref.dtype)
    for step in range(1, groups):
        part_copy(step).wait_send()


def shards(
    queries,
    key_cache,
    group_value_cache,
    coarse_keys,
    coarse_values,
    hidden,
    gate_weight,
    out_weight,
    selected,
):
    n = lax.axis_size("seq")
    groups = lax.axis_size("grp")
    ctx_dev = key_cache.shape[1]
    heads = queries.shape[1]
    width = queries.shape[2]
    vwidth = group_value_cache.shape[2]
    rows = TILE * heads
    blocks = ctx_dev // BLK
    cap = max(1, 2 * SEL // n)
    columns = out_weight.shape[1] // groups
    pieces = min(n, 8)
    wide = max(pieces, cap) * BLK

    mine = selected[0, 0]
    owners = mine // blocks
    earlier = jnp.tril(jnp.ones((SEL, SEL), jnp.int32), -1)
    rank = jnp.sum((owners[:, None] == owners[None, :]).astype(jnp.int32) * earlier, axis=1)
    slot_ids = jnp.arange(n * cap, dtype=jnp.int32)
    match = (owners * cap + rank)[:, None] == slot_ids[None, :]
    table = jnp.max(jnp.where(match, mine[:, None], -1), axis=0)
    local = jnp.maximum(table - slot_ids // cap * blocks, 0)
    request = jnp.pad(local, (0, 128 - n * cap)).reshape(1, 128)
    kpos = jnp.where(table < 0, FAR, table * BLK)[:, None] + jnp.arange(BLK, dtype=jnp.int32)
    kpos = kpos.reshape(n, 1, cap * BLK)

    vmem = pl.BlockSpec(memory_space=pltpu.VMEM)
    dma = pltpu.SemaphoreType.DMA
    bf16, f32 = jnp.bfloat16, jnp.float32
    return pl.pallas_call(
        functools.partial(kernel, n, groups, cap, width**-0.5 * math.log2(math.e)),
        out_shape=jax.ShapeDtypeStruct((TILE, columns), bf16),
        in_specs=[pl.BlockSpec(memory_space=pltpu.SMEM)]
        + [vmem] * 9
        + [pl.BlockSpec(memory_space=pl.ANY)],
        out_specs=vmem,
        scratch_shapes=[
            pltpu.VMEM((blocks, UNIT, 128), bf16),
            pltpu.VMEM((rows, 256), bf16),
            pltpu.VMEM((n, 1, 128), jnp.int32),
            pltpu.SMEM((n, 1, 128), jnp.int32),
            pltpu.VMEM((n, cap, UNIT, 128), bf16),
            pltpu.VMEM((n, cap, UNIT, 128), bf16),
            pltpu.VMEM((n, UNIT, 128), bf16),
            pltpu.VMEM((wide, 256), bf16),
            pltpu.VMEM((wide, 256), bf16),
            pltpu.VMEM((rows, 128), f32),
            pltpu.VMEM((2, rows, 128), f32),
            pltpu.VMEM((2, rows, 128), f32),
            pltpu.VMEM((TILE, heads * vwidth), bf16),
            pltpu.VMEM((groups, heads * vwidth, columns), bf16),
            pltpu.VMEM((groups, TILE, columns), bf16),
            pltpu.VMEM((groups, TILE, columns), bf16),
            pltpu.VMEM((TILE, columns), f32),
            dma((groups,)),
            dma,
            dma((n,)),
            dma((n,)),
            dma((n,)),
            dma((n,)),
            dma((n // 2,)),
            dma((n // 2,)),
            dma((n // 2,)),
            dma((n // 2,)),
            dma((groups,)),
            dma((groups,)),
        ],
        compiler_params=pltpu.CompilerParams(
            collective_id=0, has_side_effects=True, vmem_limit_bytes=60 * 1024 * 1024
        ),
    )(
        request,
        request,
        kpos,
        queries.reshape(rows, width),
        key_cache.reshape(blocks, BLK, width),
        group_value_cache.reshape(blocks, BLK, vwidth),
        coarse_keys[0],
        coarse_values[0],
        hidden,
        gate_weight[0],
        out_weight,
    )


def solution(mesh):
    return jax.shard_map(
        shards,
        mesh=mesh,
        in_specs=(
            P("seq", "grp", None),
            P("grp", "seq", None),
            P("grp", "seq", None),
            P("grp", "seq", None),
            P("grp", "seq", None),
            P("seq", None),
            P("grp", None, None),
            P("grp", None),
            P("grp", "seq", None),
        ),
        out_specs=P("seq", "grp"),
        check_vma=False,
    )
```

```python
import functools
import math

import jax
import jax.numpy as jnp
from jax import lax
from jax.experimental import pallas as pl
from jax.experimental.pallas import tpu as pltpu
from jax.sharding import PartitionSpec as P

BLK = 64
SEL = 16
TILE = 128
CSTRIDE = 16
CLEN = 32

NEGATIVE = -1e30
FAR = 1 << 28
MESH = pl.DeviceIdType.MESH
HALF = BLK // 2
UNIT = BLK + HALF + BLK


def pack(keys, values, width):
    tail = keys[:, 128:width]
    folded = jnp.concatenate([tail[:HALF], tail[HALF:]], axis=1)
    return jnp.concatenate([keys[:, :128], folded, values], axis=0)


def unpack(block):
    folded = block[BLK : BLK + HALF]
    low = lax.broadcasted_iota(jnp.int32, folded.shape, 1) < 64
    zero = jnp.zeros_like(folded)
    tails = jnp.concatenate([jnp.where(low, folded, zero), jnp.where(low, zero, folded)], axis=0)
    return jnp.concatenate([block[:BLK], tails], axis=1), block[BLK + HALF :]


def picks(read, owner, blocks, cap):
    low = owner * blocks
    found = [jnp.int32(-1)] * cap
    count = jnp.int32(0)
    for entry in range(SEL):
        block = read(entry)
        here = (block >= low) & (block < low + blocks)
        for slot in range(cap):
            found[slot] = jnp.where(here & (count == slot), block, found[slot])
        count = count + here.astype(jnp.int32)
    return found


def kernel(
    n,
    groups,
    cap,
    scale,
    own_smem,
    own_table,
    query_hbm,
    key_hbm,
    value_hbm,
    ckey_hbm,
    cvalue_hbm,
    hidden_hbm,
    gate_hbm,
    weight_hbm,
    out_ref,
    query_ref,
    key_ref,
    value_ref,
    ckey_ref,
    cvalue_ref,
    hidden_ref,
    gate_ref,
    packed,
    query_wide,
    tables,
    tables_smem,
    outgoing,
    incoming,
    coarse,
    keys_wide,
    values_wide,
    picked_top,
    picked_sum,
    picked_out,
    coarse_top,
    coarse_sum,
    coarse_out,
    attended,
    weights,
    partial,
    arrived,
    own_part,
    input_sem,
    weight_sem,
    local_sem,
    table_send,
    table_recv,
    slot_send,
    slot_recv,
    coarse_send,
    coarse_recv,
    pass_send,
    pass_recv,
    part_send,
    part_recv,
):
    me = lax.axis_index("seq")
    group = lax.axis_index("grp")
    core = lax.rem(me, 2)
    sibling = me + 1 - 2 * core
    heads, width, _ = query_ref.shape
    blocks = value_ref.shape[0]
    columns = out_ref.shape[1]
    context = blocks * BLK * n
    span = 2 * TILE

    barrier = pltpu.get_barrier_semaphore()

    def greet(step, carry):
        pl.semaphore_signal(
            barrier, inc=1, device_id={"seq": lax.rem(me + step, n)}, device_id_type=MESH
        )
        return carry

    lax.fori_loop(1, n, greet, 0)
    for step in range(1, groups):
        pl.semaphore_signal(
            barrier, inc=1, device_id={"grp": lax.rem(group + step, groups)}, device_id_type=MESH
        )

    loads = [
        pltpu.make_async_copy(source, target, input_sem.at[index])
        for index, (source, target) in enumerate(
            [
                (ckey_hbm, ckey_ref),
                (cvalue_hbm, cvalue_ref),
                (key_hbm, key_ref),
                (value_hbm, value_ref),
                (query_hbm, query_ref),
                (hidden_hbm, hidden_ref),
                (gate_hbm, gate_ref),
            ]
        )
    ]
    for load in loads:
        load.start()

    def weight_copy(step):
        target = lax.rem(group + step, groups)
        return pltpu.make_async_copy(
            weight_hbm.at[:, pl.ds(pl.multiple_of(target * columns, 128), columns)],
            weights.at[step],
            weight_sem.at[step],
        )

    for step in range(groups):
        weight_copy(step).start()

    loads[0].wait()
    loads[1].wait()
    coarse[me] = pack(ckey_ref[...], cvalue_ref[...], width)
    loads[2].wait()
    loads[3].wait()
    for pair in range(blocks // 2):
        both = key_ref[:, pair * 128 : (pair + 1) * 128].T
        packed[2 * pair] = pack(both[:BLK], value_ref[2 * pair], width)
        packed[2 * pair + 1] = pack(both[BLK:], value_ref[2 * pair + 1], width)
    pl.semaphore_wait(barrier, n - 1 + groups - 1)

    def table_copy(step):
        return pltpu.make_async_remote_copy(
            src_ref=own_table,
            dst_ref=tables.at[step],
            send_sem=table_send.at[step],
            recv_sem=table_recv.at[step],
            device_id={"seq": lax.rem(me + step, n)},
            device_id_type=MESH,
        )

    def coarse_copy(step):
        return pltpu.make_async_remote_copy(
            src_ref=coarse.at[me],
            dst_ref=coarse.at[me],
            send_sem=coarse_send.at[step],
            recv_sem=coarse_recv.at[step],
            device_id={"seq": lax.rem(me + 2 * step, n)},
            device_id_type=MESH,
        )

    def pass_copy(step):
        origin = lax.rem(me - 2 * step + n, n)
        return pltpu.make_async_remote_copy(
            src_ref=coarse.at[origin],
            dst_ref=coarse.at[origin],
            send_sem=pass_send.at[step],
            recv_sem=pass_recv.at[step],
            device_id={"seq": sibling},
            device_id_type=MESH,
        )

    def slot_copy(step):
        return pltpu.make_async_remote_copy(
            src_ref=outgoing.at[step],
            dst_ref=incoming.at[step],
            send_sem=slot_send.at[step],
            recv_sem=slot_recv.at[step],
            device_id={"seq": lax.rem(me + step, n)},
            device_id_type=MESH,
        )

    def turn(index):
        return n // 2 + (index // 2) * (1 - 2 * lax.rem(index, 2))

    def send_table(step, carry):
        table_copy(step).start()
        return carry

    lax.fori_loop(1, n, send_table, 0)

    def send_coarse(step, carry):
        coarse_copy(step).start()
        return carry

    lax.fori_loop(1, n // 2, send_coarse, 0)
    pass_copy(0).start()

    def wait_table(step, carry):
        table_copy(step).wait_recv()
        return carry

    lax.fori_loop(1, n, wait_table, 0)
    to_smem = pltpu.make_async_copy(tables, tables_smem, local_sem)
    to_smem.start()
    to_smem.wait()

    def send_slots(index, carry):
        step = turn(index)
        wanted = picks(lambda entry: tables_smem[n - step, 0, 0, entry], me, blocks, cap)
        for slot in range(cap):
            outgoing[step, slot] = packed[jnp.maximum(wanted[slot] - me * blocks, 0)]
        slot_copy(step).start()
        return carry

    lax.fori_loop(1, n, send_slots, 0)

    loads[4].wait()
    for head in range(heads):
        one = query_ref[head]
        query_wide[:width, head * 128 : (head + 1) * 128] = one
        query_wide[width:, head * 128 : (head + 1) * 128] = one[128:]

    first_pos = context - TILE * n + me * TILE
    row = lax.broadcasted_iota(jnp.int32, (BLK, span), 0)
    query = lax.rem(lax.broadcasted_iota(jnp.int32, (BLK, span), 1), TILE)

    def fill(place, block):
        keys, values = unpack(block)
        keys_wide[place * BLK : (place + 1) * BLK] = keys
        return values

    def attend(count, bounds, stride, top_ref, sum_ref, out, first):
        lag = row * stride - query

        def chunk(index, carry):
            here = pl.ds(pl.multiple_of(index * span, span), span)
            scores = jnp.dot(
                keys_wide[: count * BLK], query_wide[:, here], preferred_element_type=jnp.float32
            )
            scores = jnp.concatenate(
                [
                    jnp.where(lag <= bounds[block], scores[block * BLK : (block + 1) * BLK], -jnp.inf)
                    for block in range(count)
                ],
                axis=0,
            )
            top = jnp.max(scores, axis=0, keepdims=True)
            if first:
                new = jnp.maximum(top, NEGATIVE)
            else:
                old = top_ref[:, here]
                new = jnp.maximum(old, top)
                factor = jnp.exp2((old - new) * scale)
            exponents = jnp.exp2((scores - new) * scale).astype(jnp.bfloat16)
            added = jnp.dot(
                values_wide[:, : count * BLK], exponents, preferred_element_type=jnp.float32
            )
            if first:
                out[:, here] = added[:128]
                sum_ref[:, here] = added[128:129]
            else:
                out[:, here] = out[:, here] * factor + added[:128]
                sum_ref[:, here] = sum_ref[:, here] * factor + added[128:129]
            top_ref[:, here] = new
            return carry

        lax.fori_loop(0, heads * TILE // span, chunk, 0, unroll=4)

    values_wide[128:, :] = jnp.ones_like(values_wide[128:, :])

    def attend_picked(owner, group_of, first):
        wanted = picks(lambda entry: own_smem[0, 0, entry], owner, blocks, cap)
        values = [fill(slot, group_of[slot]) for slot in range(cap)]
        values_wide[:128, : cap * BLK] = jnp.concatenate(values, axis=0).T
        bounds = [
            jnp.where(wanted[slot] < 0, -FAR, first_pos - wanted[slot] * BLK) for slot in range(cap)
        ]
        attend(cap, bounds, 1, picked_top, picked_sum, picked_out, first)

    mine = picks(lambda entry: own_smem[0, 0, entry], me, blocks, cap)
    attend_picked(me, [packed[jnp.maximum(block - me * blocks, 0)] for block in mine], True)

    loads[5].wait()
    loads[6].wait()
    gates = jax.nn.sigmoid(
        lax.dot_general(
            gate_ref[...],
            hidden_ref[...],
            (((1,), (1,)), ((), ())),
            preferred_element_type=jnp.float32,
        )
    )

    def forward(step, carry):
        coarse_copy(step).wait_recv()
        pass_copy(step).start()
        return carry

    lax.fori_loop(1, n // 2, forward, 0)

    def passed(step, carry):
        pass_copy(step).wait_recv()
        return carry

    lax.fori_loop(0, n // 2, passed, 0)

    pieces = min(n, 8)

    def coarse_step(index, first):
        values = [fill(piece, coarse[index * pieces + piece]) for piece in range(pieces)]
        values_wide[:128, : pieces * BLK] = jnp.concatenate(values, axis=0).T
        start = first_pos - (CLEN - 1) - index * (pieces * BLK * CSTRIDE)
        bounds = [start - piece * (BLK * CSTRIDE) for piece in range(pieces)]
        attend(pieces, bounds, CSTRIDE, coarse_top, coarse_sum, coarse_out, first)

    coarse_step(0, True)
    if n > pieces:

        def coarse_more(index, carry):
            coarse_step(index, False)
            return carry

        lax.fori_loop(1, n // pieces, coarse_more, 0)

    def picked_step(index, carry):
        step = turn(index)
        slot_copy(step).wait_recv()
        owner = lax.rem(me - step + n, n)
        attend_picked(owner, [incoming[step, slot] for slot in range(cap)], False)
        return carry

    lax.fori_loop(1, n, picked_step, 0)

    for head in range(heads):
        here = slice(head * 128, (head + 1) * 128)
        of_coarse = gates[head : head + 1] / coarse_sum[:, here]
        of_picked = gates[heads + head : heads + head + 1] / picked_sum[:, here]
        mixed = coarse_out[:, here] * of_coarse + picked_out[:, here] * of_picked
        attended[:, here] = mixed.T.astype(jnp.bfloat16)

    def part_copy(step):
        return pltpu.make_async_remote_copy(
            src_ref=partial.at[step],
            dst_ref=arrived.at[step],
            send_sem=part_send.at[step],
            recv_sem=part_recv.at[step],
            device_id={"grp": lax.rem(group + step, groups)},
            device_id_type=MESH,
        )

    for step in range(1, groups):
        weight_copy(step).wait()
        partial[step] = jnp.dot(
            attended[...], weights[step], preferred_element_type=jnp.float32
        ).astype(jnp.bfloat16)
        part_copy(step).start()
    weight_copy(0).wait()
    own_part[...] = jnp.dot(attended[...], weights[0], preferred_element_type=jnp.float32)

    def sent(step, carry):
        table_copy(step).wait_send()
        slot_copy(step).wait_send()
        return carry

    lax.fori_loop(1, n, sent, 0)

    def sent_coarse(step, carry):
        coarse_copy(step).wait_send()
        pass_copy(step).wait_send()
        return carry

    lax.fori_loop(1, n // 2, sent_coarse, 0)
    pass_copy(0).wait_send()
    total = own_part[...]
    for step in range(1, groups):
        part_copy(step).wait_recv()
        total = total + arrived[step].astype(jnp.float32)
    out_ref[...] = total.astype(out_ref.dtype)
    for step in range(1, groups):
        part_copy(step).wait_send()


def shards(
    queries,
    key_cache,
    group_value_cache,
    coarse_keys,
    coarse_values,
    hidden,
    gate_weight,
    out_weight,
    selected,
):
    n = lax.axis_size("seq")
    groups = lax.axis_size("grp")
    ctx_dev = key_cache.shape[1]
    heads = queries.shape[1]
    width = queries.shape[2]
    vwidth = group_value_cache.shape[2]
    rows = TILE * heads
    blocks = ctx_dev // BLK
    cap = max(1, 2 * SEL // n)
    columns = out_weight.shape[1] // groups
    pieces = min(n, 8)
    wide = max(pieces, cap) * BLK

    vmem = pl.BlockSpec(memory_space=pltpu.VMEM)
    hbm = pl.BlockSpec(memory_space=pl.ANY)
    dma = pltpu.SemaphoreType.DMA
    bf16, f32 = jnp.bfloat16, jnp.float32
    inputs = (
        queries.transpose(1, 2, 0),
        key_cache[0].T,
        group_value_cache.reshape(blocks, BLK, vwidth),
        coarse_keys[0],
        coarse_values[0],
        hidden,
        gate_weight[0].T,
    )
    return pl.pallas_call(
        functools.partial(kernel, n, groups, cap, width**-0.5 * math.log2(math.e)),
        out_shape=jax.ShapeDtypeStruct((TILE, columns), bf16),
        in_specs=[pl.BlockSpec(memory_space=pltpu.SMEM), vmem] + [hbm] * (len(inputs) + 1),
        out_specs=vmem,
        scratch_shapes=[pltpu.VMEM(one.shape, bf16) for one in inputs]
        + [
            pltpu.VMEM((blocks, UNIT, 128), bf16),
            pltpu.VMEM((256, rows), bf16),
            pltpu.VMEM((n, 1, 1, SEL), jnp.int32),
            pltpu.SMEM((n, 1, 1, SEL), jnp.int32),
            pltpu.VMEM((n, cap, UNIT, 128), bf16),
            pltpu.VMEM((n, cap, UNIT, 128), bf16),
            pltpu.VMEM((n, UNIT, 128), bf16),
            pltpu.VMEM((wide, 256), bf16),
            pltpu.VMEM((144, wide), bf16),
            pltpu.VMEM((1, rows), f32),
            pltpu.VMEM((1, rows), f32),
            pltpu.VMEM((vwidth, rows), f32),
            pltpu.VMEM((1, rows), f32),
            pltpu.VMEM((1, rows), f32),
            pltpu.VMEM((vwidth, rows), f32),
            pltpu.VMEM((TILE, heads * vwidth), bf16),
            pltpu.VMEM((groups, heads * vwidth, columns), bf16),
            pltpu.VMEM((groups, TILE, columns), bf16),
            pltpu.VMEM((groups, TILE, columns), bf16),
            pltpu.VMEM((TILE, columns), f32),
            dma((len(inputs),)),
            dma((groups,)),
            dma,
            dma((n,)),
            dma((n,)),
            dma((n,)),
            dma((n,)),
            dma((n // 2,)),
            dma((n // 2,)),
            dma((n // 2,)),
            dma((n // 2,)),
            dma((groups,)),
            dma((groups,)),
        ],
        compiler_params=pltpu.CompilerParams(
            collective_id=0, has_side_effects=True, vmem_limit_bytes=60 * 1024 * 1024
        ),
    )(selected, selected, *inputs, out_weight)


def solution(mesh):
    return jax.shard_map(
        shards,
        mesh=mesh,
        in_specs=(
            P("seq", "grp", None),
            P("grp", "seq", None),
            P("grp", "seq", None),
            P("grp", "seq", None),
            P("grp", "seq", None),
            P("seq", None),
            P("grp", None, None),
            P("grp", None),
            P("grp", "seq", None),
        ),
        out_specs=P("seq", "grp"),
        check_vma=False,
    )
```

```python
import functools
import math

import jax
import jax.numpy as jnp
from jax import lax
from jax.experimental import pallas as pl
from jax.experimental.pallas import tpu as pltpu
from jax.sharding import PartitionSpec as P

BLK = 64
SEL = 16
TILE = 128
CSTRIDE = 16
CLEN = 32

NEGATIVE = -1e30
FAR = 1 << 28
MESH = pl.DeviceIdType.MESH
HALF = BLK // 2
UNIT = BLK + HALF + BLK


def pack(keys, values, width):
    tail = keys[:, 128:width]
    folded = jnp.concatenate([tail[:HALF], tail[HALF:]], axis=1)
    return jnp.concatenate([keys[:, :128], folded, values], axis=0)


def unpack(block):
    folded = block[BLK : BLK + HALF]
    low = lax.broadcasted_iota(jnp.int32, folded.shape, 1) < 64
    zero = jnp.zeros_like(folded)
    tails = jnp.concatenate([jnp.where(low, folded, zero), jnp.where(low, zero, folded)], axis=0)
    return jnp.concatenate([block[:BLK], tails], axis=1), block[BLK + HALF :]


def flip(index, step, size):
    shared = 0
    bit = 1
    while bit < size:
        shared = shared + lax.rem(index // bit, 2) * (step // bit % 2) * bit
        bit *= 2
    return index + step - 2 * shared


def picks(read, owner, blocks, cap):
    low = owner * blocks
    found = [jnp.int32(-1)] * cap
    count = jnp.int32(0)
    for entry in range(SEL):
        block = read(entry)
        here = (block >= low) & (block < low + blocks)
        for slot in range(cap):
            found[slot] = jnp.where(here & (count == slot), block, found[slot])
        count = count + here.astype(jnp.int32)
    return found


def kernel(
    n,
    groups,
    cap,
    scale,
    own_smem,
    own_table,
    query_hbm,
    key_hbm,
    value_hbm,
    ckey_hbm,
    cvalue_hbm,
    hidden_hbm,
    gate_hbm,
    weight_hbm,
    out_ref,
    query_ref,
    key_ref,
    value_ref,
    ckey_ref,
    cvalue_ref,
    hidden_ref,
    gate_ref,
    packed,
    query_wide,
    tables,
    tables_smem,
    outgoing,
    incoming,
    coarse,
    keys_wide,
    values_wide,
    picked_top,
    picked_sum,
    picked_out,
    coarse_top,
    coarse_sum,
    coarse_out,
    attended,
    weights,
    partial,
    arrived,
    own_part,
    input_sem,
    weight_sem,
    local_sem,
    table_send,
    table_recv,
    slot_send,
    slot_recv,
    coarse_send,
    coarse_recv,
    pass_send,
    pass_recv,
    part_send,
    part_recv,
):
    me = lax.axis_index("seq")
    group = lax.axis_index("grp")
    core = lax.rem(me, 2)
    sibling = me + 1 - 2 * core
    heads, width, _ = query_ref.shape
    blocks = value_ref.shape[0]
    columns = out_ref.shape[1]
    context = blocks * BLK * n
    span = 2 * TILE

    barrier = pltpu.get_barrier_semaphore()

    def greet(step, carry):
        pl.semaphore_signal(
            barrier, inc=1, device_id={"seq": flip(me, step, n)}, device_id_type=MESH
        )
        return carry

    lax.fori_loop(1, n, greet, 0)
    for step in range(1, groups):
        pl.semaphore_signal(
            barrier, inc=1, device_id={"grp": flip(group, step, groups)}, device_id_type=MESH
        )

    loads = [
        pltpu.make_async_copy(source, target, input_sem.at[index])
        for index, (source, target) in enumerate(
            [
                (ckey_hbm, ckey_ref),
                (cvalue_hbm, cvalue_ref),
                (key_hbm, key_ref),
                (value_hbm, value_ref),
                (query_hbm, query_ref),
                (hidden_hbm, hidden_ref),
                (gate_hbm, gate_ref),
            ]
        )
    ]
    for load in loads:
        load.start()

    def weight_copy(step):
        target = flip(group, step, groups)
        return pltpu.make_async_copy(
            weight_hbm.at[:, pl.ds(pl.multiple_of(target * columns, 128), columns)],
            weights.at[step],
            weight_sem.at[step],
        )

    for step in reversed(range(groups)):
        weight_copy(step).start()

    loads[0].wait()
    loads[1].wait()
    coarse[me] = pack(ckey_ref[...], cvalue_ref[...], width)
    loads[2].wait()
    loads[3].wait()
    for pair in range(blocks // 2):
        both = key_ref[:, pair * 128 : (pair + 1) * 128].T
        packed[2 * pair] = pack(both[:BLK], value_ref[2 * pair], width)
        packed[2 * pair + 1] = pack(both[BLK:], value_ref[2 * pair + 1], width)
    pl.semaphore_wait(barrier, n - 1 + groups - 1)

    def table_copy(step):
        return pltpu.make_async_remote_copy(
            src_ref=own_table,
            dst_ref=tables.at[step],
            send_sem=table_send.at[step],
            recv_sem=table_recv.at[step],
            device_id={"seq": flip(me, step, n)},
            device_id_type=MESH,
        )

    def coarse_copy(step):
        return pltpu.make_async_remote_copy(
            src_ref=coarse.at[me],
            dst_ref=coarse.at[me],
            send_sem=coarse_send.at[step],
            recv_sem=coarse_recv.at[step],
            device_id={"seq": flip(me, 2 * step, n)},
            device_id_type=MESH,
        )

    def pass_copy(step):
        origin = flip(me, 2 * step, n)
        return pltpu.make_async_remote_copy(
            src_ref=coarse.at[origin],
            dst_ref=coarse.at[origin],
            send_sem=pass_send.at[step],
            recv_sem=pass_recv.at[step],
            device_id={"seq": sibling},
            device_id_type=MESH,
        )

    def slot_copy(step):
        return pltpu.make_async_remote_copy(
            src_ref=outgoing.at[step],
            dst_ref=incoming.at[step],
            send_sem=slot_send.at[step],
            recv_sem=slot_recv.at[step],
            device_id={"seq": flip(me, step, n)},
            device_id_type=MESH,
        )

    def send_table(step, carry):
        table_copy(step).start()
        return carry

    lax.fori_loop(1, n, send_table, 0)

    def send_coarse(step, carry):
        coarse_copy(step).start()
        return carry

    lax.fori_loop(1, n // 2, send_coarse, 0)
    pass_copy(0).start()

    def wait_table(step, carry):
        table_copy(step).wait_recv()
        return carry

    lax.fori_loop(1, n, wait_table, 0)
    to_smem = pltpu.make_async_copy(tables, tables_smem, local_sem)
    to_smem.start()
    to_smem.wait()

    def send_slots(step, carry):
        wanted = picks(lambda entry: tables_smem[step, 0, 0, entry], me, blocks, cap)
        for slot in range(cap):
            outgoing[step, slot] = packed[jnp.maximum(wanted[slot] - me * blocks, 0)]
        slot_copy(step).start()
        return carry

    lax.fori_loop(1, n, send_slots, 0)

    loads[4].wait()
    for head in range(heads):
        one = query_ref[head]
        query_wide[:width, head * 128 : (head + 1) * 128] = one
        query_wide[width:, head * 128 : (head + 1) * 128] = one[128:]

    first_pos = context - TILE * n + me * TILE
    row = lax.broadcasted_iota(jnp.int32, (BLK, span), 0)
    query = lax.rem(lax.broadcasted_iota(jnp.int32, (BLK, span), 1), TILE)

    def fill(place, block):
        keys, values = unpack(block)
        keys_wide[place * BLK : (place + 1) * BLK] = keys
        return values

    def attend(count, bounds, stride, top_ref, sum_ref, out, first):
        lag = row * stride - query

        def chunk(index, carry):
            here = pl.ds(pl.multiple_of(index * span, span), span)
            scores = jnp.dot(
                keys_wide[: count * BLK], query_wide[:, here], preferred_element_type=jnp.float32
            )
            scores = jnp.concatenate(
                [
                    jnp.where(lag <= bounds[block], scores[block * BLK : (block + 1) * BLK], -jnp.inf)
                    for block in range(count)
                ],
                axis=0,
            )
            top = jnp.max(scores, axis=0, keepdims=True)
            if first:
                new = jnp.maximum(top, NEGATIVE)
            else:
                old = top_ref[:, here]
                new = jnp.maximum(old, top)
                factor = jnp.exp2((old - new) * scale)
            exponents = jnp.exp2((scores - new) * scale).astype(jnp.bfloat16)
            added = jnp.dot(
                values_wide[:, : count * BLK], exponents, preferred_element_type=jnp.float32
            )
            if first:
                out[:, here] = added[:128]
                sum_ref[:, here] = added[128:129]
            else:
                out[:, here] = out[:, here] * factor + added[:128]
                sum_ref[:, here] = sum_ref[:, here] * factor + added[128:129]
            top_ref[:, here] = new
            return carry

        lax.fori_loop(0, heads * TILE // span, chunk, 0, unroll=4)

    values_wide[128:, :] = jnp.ones_like(values_wide[128:, :])

    def attend_picked(owner, group_of, first):
        wanted = picks(lambda entry: own_smem[0, 0, entry], owner, blocks, cap)
        values = [fill(slot, group_of[slot]) for slot in range(cap)]
        values_wide[:128, : cap * BLK] = jnp.concatenate(values, axis=0).T
        bounds = [
            jnp.where(wanted[slot] < 0, -FAR, first_pos - wanted[slot] * BLK) for slot in range(cap)
        ]
        attend(cap, bounds, 1, picked_top, picked_sum, picked_out, first)

    mine = picks(lambda entry: own_smem[0, 0, entry], me, blocks, cap)
    attend_picked(me, [packed[jnp.maximum(block - me * blocks, 0)] for block in mine], True)

    loads[5].wait()
    loads[6].wait()
    gates = jax.nn.sigmoid(
        lax.dot_general(
            gate_ref[...],
            hidden_ref[...],
            (((1,), (1,)), ((), ())),
            preferred_element_type=jnp.float32,
        )
    )

    def forward(step, carry):
        coarse_copy(step).wait_recv()
        pass_copy(step).start()
        return carry

    lax.fori_loop(1, n // 2, forward, 0)

    def passed(step, carry):
        pass_copy(step).wait_recv()
        return carry

    lax.fori_loop(0, n // 2, passed, 0)

    pieces = min(n, 8)

    def coarse_step(index, first):
        values = [fill(piece, coarse[index * pieces + piece]) for piece in range(pieces)]
        values_wide[:128, : pieces * BLK] = jnp.concatenate(values, axis=0).T
        start = first_pos - (CLEN - 1) - index * (pieces * BLK * CSTRIDE)
        bounds = [start - piece * (BLK * CSTRIDE) for piece in range(pieces)]
        attend(pieces, bounds, CSTRIDE, coarse_top, coarse_sum, coarse_out, first)

    coarse_step(0, True)
    if n > pieces:

        def coarse_more(index, carry):
            coarse_step(index, False)
            return carry

        lax.fori_loop(1, n // pieces, coarse_more, 0)

    def picked_step(step, carry):
        slot_copy(step).wait_recv()
        owner = flip(me, step, n)
        attend_picked(owner, [incoming[step, slot] for slot in range(cap)], False)
        return carry

    lax.fori_loop(1, n, picked_step, 0)

    for head in range(heads):
        here = slice(head * 128, (head + 1) * 128)
        of_coarse = gates[head : head + 1] / coarse_sum[:, here]
        of_picked = gates[heads + head : heads + head + 1] / picked_sum[:, here]
        mixed = coarse_out[:, here] * of_coarse + picked_out[:, here] * of_picked
        attended[:, here] = mixed.T.astype(jnp.bfloat16)

    def part_copy(step):
        return pltpu.make_async_remote_copy(
            src_ref=partial.at[step],
            dst_ref=arrived.at[step],
            send_sem=part_send.at[step],
            recv_sem=part_recv.at[step],
            device_id={"grp": flip(group, step, groups)},
            device_id_type=MESH,
        )

    for step in reversed(range(1, groups)):
        weight_copy(step).wait()
        partial[step] = jnp.dot(
            attended[...], weights[step], preferred_element_type=jnp.float32
        ).astype(jnp.bfloat16)
        part_copy(step).start()
    weight_copy(0).wait()
    own_part[...] = jnp.dot(attended[...], weights[0], preferred_element_type=jnp.float32)

    def sent(step, carry):
        table_copy(step).wait_send()
        slot_copy(step).wait_send()
        return carry

    lax.fori_loop(1, n, sent, 0)

    def sent_coarse(step, carry):
        coarse_copy(step).wait_send()
        pass_copy(step).wait_send()
        return carry

    lax.fori_loop(1, n // 2, sent_coarse, 0)
    pass_copy(0).wait_send()
    total = own_part[...]
    for step in range(1, groups):
        part_copy(step).wait_recv()
        total = total + arrived[step].astype(jnp.float32)
    out_ref[...] = total.astype(out_ref.dtype)
    for step in range(1, groups):
        part_copy(step).wait_send()


def shards(
    queries,
    key_cache,
    group_value_cache,
    coarse_keys,
    coarse_values,
    hidden,
    gate_weight,
    out_weight,
    selected,
):
    n = lax.axis_size("seq")
    groups = lax.axis_size("grp")
    ctx_dev = key_cache.shape[1]
    heads = queries.shape[1]
    width = queries.shape[2]
    vwidth = group_value_cache.shape[2]
    rows = TILE * heads
    blocks = ctx_dev // BLK
    cap = max(1, 2 * SEL // n)
    columns = out_weight.shape[1] // groups
    pieces = min(n, 8)
    wide = max(pieces, cap) * BLK

    vmem = pl.BlockSpec(memory_space=pltpu.VMEM)
    hbm = pl.BlockSpec(memory_space=pl.ANY)
    dma = pltpu.SemaphoreType.DMA
    bf16, f32 = jnp.bfloat16, jnp.float32
    inputs = (
        queries.transpose(1, 2, 0),
        key_cache[0].T,
        group_value_cache.reshape(blocks, BLK, vwidth),
        coarse_keys[0],
        coarse_values[0],
        hidden,
        gate_weight[0].T,
    )
    return pl.pallas_call(
        functools.partial(kernel, n, groups, cap, width**-0.5 * math.log2(math.e)),
        out_shape=jax.ShapeDtypeStruct((TILE, columns), bf16),
        in_specs=[pl.BlockSpec(memory_space=pltpu.SMEM), vmem] + [hbm] * (len(inputs) + 1),
        out_specs=vmem,
        scratch_shapes=[pltpu.VMEM(one.shape, bf16) for one in inputs]
        + [
            pltpu.VMEM((blocks, UNIT, 128), bf16),
            pltpu.VMEM((256, rows), bf16),
            pltpu.VMEM((n, 1, 1, SEL), jnp.int32),
            pltpu.SMEM((n, 1, 1, SEL), jnp.int32),
            pltpu.VMEM((n, cap, UNIT, 128), bf16),
            pltpu.VMEM((n, cap, UNIT, 128), bf16),
            pltpu.VMEM((n, UNIT, 128), bf16),
            pltpu.VMEM((wide, 256), bf16),
            pltpu.VMEM((144, wide), bf16),
            pltpu.VMEM((1, rows), f32),
            pltpu.VMEM((1, rows), f32),
            pltpu.VMEM((vwidth, rows), f32),
            pltpu.VMEM((1, rows), f32),
            pltpu.VMEM((1, rows), f32),
            pltpu.VMEM((vwidth, rows), f32),
            pltpu.VMEM((TILE, heads * vwidth), bf16),
            pltpu.VMEM((groups, heads * vwidth, columns), bf16),
            pltpu.VMEM((groups, TILE, columns), bf16),
            pltpu.VMEM((groups, TILE, columns), bf16),
            pltpu.VMEM((TILE, columns), f32),
            dma((len(inputs),)),
            dma((groups,)),
            dma,
            dma((n,)),
            dma((n,)),
            dma((n,)),
            dma((n,)),
            dma((n // 2,)),
            dma((n // 2,)),
            dma((n // 2,)),
            dma((n // 2,)),
            dma((groups,)),
            dma((groups,)),
        ],
        compiler_params=pltpu.CompilerParams(
            collective_id=0, has_side_effects=True, vmem_limit_bytes=60 * 1024 * 1024
        ),
    )(selected, selected, *inputs, out_weight)


def solution(mesh):
    return jax.shard_map(
        shards,
        mesh=mesh,
        in_specs=(
            P("seq", "grp", None),
            P("grp", "seq", None),
            P("grp", "seq", None),
            P("grp", "seq", None),
            P("grp", "seq", None),
            P("seq", None),
            P("grp", None, None),
            P("grp", None),
            P("grp", "seq", None),
        ),
        out_specs=P("seq", "grp"),
        check_vma=False,
    )
```

```python
import functools
import math

import jax
import jax.numpy as jnp
from jax import lax
from jax.experimental import pallas as pl
from jax.experimental.pallas import tpu as pltpu
from jax.sharding import PartitionSpec as P

BLK = 64
SEL = 16
TILE = 128
CSTRIDE = 16
CLEN = 32

NEGATIVE = -1e30
FAR = 1 << 28
MESH = pl.DeviceIdType.MESH
HALF = BLK // 2
UNIT = BLK + HALF + BLK


def pack(keys, values, width):
    tail = keys[:, 128:width]
    folded = jnp.concatenate([tail[:HALF], tail[HALF:]], axis=1)
    return jnp.concatenate([keys[:, :128], folded, values], axis=0)


def unpack(block):
    folded = block[BLK : BLK + HALF]
    low = lax.broadcasted_iota(jnp.int32, folded.shape, 1) < 64
    zero = jnp.zeros_like(folded)
    tails = jnp.concatenate([jnp.where(low, folded, zero), jnp.where(low, zero, folded)], axis=0)
    return jnp.concatenate([block[:BLK], tails], axis=1), block[BLK + HALF :]


def flip(index, step, size):
    shared = 0
    bit = 1
    while bit < size:
        shared = shared + lax.rem(index // bit, 2) * (step // bit % 2) * bit
        bit *= 2
    return index + step - 2 * shared


def picks(read, owner, blocks, cap):
    low = owner * blocks
    found = [jnp.int32(-1)] * cap
    count = jnp.int32(0)
    for entry in range(SEL):
        block = read(entry)
        here = (block >= low) & (block < low + blocks)
        for slot in range(cap):
            found[slot] = jnp.where(here & (count == slot), block, found[slot])
        count = count + here.astype(jnp.int32)
    return found


def kernel(
    n,
    groups,
    cap,
    scale,
    own_smem,
    own_table,
    query_hbm,
    key_hbm,
    value_hbm,
    ckey_hbm,
    cvalue_hbm,
    hidden_hbm,
    gate_hbm,
    weight_hbm,
    out_ref,
    query_ref,
    key_ref,
    value_ref,
    ckey_ref,
    cvalue_ref,
    hidden_ref,
    gate_ref,
    packed,
    query_wide,
    tables,
    tables_smem,
    outgoing,
    incoming,
    coarse,
    keys_wide,
    values_wide,
    picked_top,
    picked_sum,
    picked_out,
    coarse_top,
    coarse_sum,
    coarse_out,
    attended,
    weights,
    partial,
    arrived,
    own_part,
    input_sem,
    weight_sem,
    local_sem,
    table_send,
    table_recv,
    slot_send,
    slot_recv,
    coarse_send,
    coarse_recv,
    pass_send,
    pass_recv,
    part_send,
    part_recv,
):
    me = lax.axis_index("seq")
    group = lax.axis_index("grp")
    core = lax.rem(me, 2)
    sibling = me + 1 - 2 * core
    heads, width, _ = query_ref.shape
    blocks = value_ref.shape[0]
    columns = out_ref.shape[1]
    context = blocks * BLK * n
    span = 2 * TILE

    barrier = pltpu.get_barrier_semaphore()

    def greet(step, carry):
        pl.semaphore_signal(
            barrier, inc=1, device_id={"seq": flip(me, step, n)}, device_id_type=MESH
        )
        return carry

    lax.fori_loop(1, n, greet, 0)
    for step in range(1, groups):
        pl.semaphore_signal(
            barrier, inc=1, device_id={"grp": flip(group, step, groups)}, device_id_type=MESH
        )

    loads = [
        pltpu.make_async_copy(source, target, input_sem.at[index])
        for index, (source, target) in enumerate(
            [
                (ckey_hbm, ckey_ref),
                (cvalue_hbm, cvalue_ref),
                (key_hbm, key_ref),
                (value_hbm, value_ref),
                (query_hbm, query_ref),
                (hidden_hbm, hidden_ref),
                (gate_hbm, gate_ref),
            ]
        )
    ]
    for load in loads:
        load.start()

    def weight_copy(step):
        target = flip(group, step, groups)
        return pltpu.make_async_copy(
            weight_hbm.at[:, pl.ds(pl.multiple_of(target * columns, 128), columns)],
            weights.at[step],
            weight_sem.at[step],
        )

    for step in reversed(range(groups)):
        weight_copy(step).start()

    loads[0].wait()
    loads[1].wait()
    coarse[me] = pack(ckey_ref[...], cvalue_ref[...], width)
    loads[2].wait()
    loads[3].wait()
    for pair in range(blocks // 2):
        both = key_ref[:, pair * 128 : (pair + 1) * 128].T
        packed[2 * pair] = pack(both[:BLK], value_ref[2 * pair], width)
        packed[2 * pair + 1] = pack(both[BLK:], value_ref[2 * pair + 1], width)
    pl.semaphore_wait(barrier, n - 1 + groups - 1)

    def table_copy(step):
        return pltpu.make_async_remote_copy(
            src_ref=own_table,
            dst_ref=tables.at[step],
            send_sem=table_send.at[step],
            recv_sem=table_recv.at[step],
            device_id={"seq": flip(me, step, n)},
            device_id_type=MESH,
        )

    def coarse_copy(step):
        return pltpu.make_async_remote_copy(
            src_ref=coarse.at[me],
            dst_ref=coarse.at[me],
            send_sem=coarse_send.at[step],
            recv_sem=coarse_recv.at[step],
            device_id={"seq": flip(me, 2 * step, n)},
            device_id_type=MESH,
        )

    def pass_copy(step):
        origin = flip(me, 2 * step, n)
        return pltpu.make_async_remote_copy(
            src_ref=coarse.at[origin],
            dst_ref=coarse.at[origin],
            send_sem=pass_send.at[step],
            recv_sem=pass_recv.at[step],
            device_id={"seq": sibling},
            device_id_type=MESH,
        )

    def slot_copy(step):
        return pltpu.make_async_remote_copy(
            src_ref=outgoing.at[step],
            dst_ref=incoming.at[step],
            send_sem=slot_send.at[step],
            recv_sem=slot_recv.at[step],
            device_id={"seq": flip(me, step, n)},
            device_id_type=MESH,
        )

    def send_table(step, carry):
        table_copy(step).start()
        return carry

    lax.fori_loop(1, n, send_table, 0)

    def send_coarse(step, carry):
        coarse_copy(step).start()
        return carry

    lax.fori_loop(1, n // 2, send_coarse, 0)
    pass_copy(0).start()

    def wait_table(step, carry):
        table_copy(step).wait_recv()
        return carry

    lax.fori_loop(1, n, wait_table, 0)
    to_smem = pltpu.make_async_copy(tables, tables_smem, local_sem)
    to_smem.start()
    to_smem.wait()

    def send_slots(step, carry):
        wanted = picks(lambda entry: tables_smem[step, 0, 0, entry], me, blocks, cap)
        for slot in range(cap):
            outgoing[step, slot] = packed[jnp.maximum(wanted[slot] - me * blocks, 0)]
        slot_copy(step).start()
        return carry

    lax.fori_loop(1, n, send_slots, 0)

    loads[4].wait()
    for head in range(heads):
        one = query_ref[head]
        query_wide[:width, head * 128 : (head + 1) * 128] = one
        query_wide[width:, head * 128 : (head + 1) * 128] = one[128:]

    first_pos = context - TILE * n + me * TILE
    row = lax.broadcasted_iota(jnp.int32, (BLK, span), 0)
    query = lax.rem(lax.broadcasted_iota(jnp.int32, (BLK, span), 1), TILE)

    def fill(place, block):
        keys, values = unpack(block)
        keys_wide[place * BLK : (place + 1) * BLK] = keys
        return values

    def attend(count, bounds, stride, top_ref, sum_ref, out, first):
        lag = row * stride - query

        def chunk(index, carry):
            here = pl.ds(pl.multiple_of(index * span, span), span)
            scores = jnp.dot(
                keys_wide[: count * BLK], query_wide[:, here], preferred_element_type=jnp.float32
            )
            scores = jnp.concatenate(
                [
                    jnp.where(lag <= bounds[block], scores[block * BLK : (block + 1) * BLK], -jnp.inf)
                    for block in range(count)
                ],
                axis=0,
            )
            top = jnp.max(scores, axis=0, keepdims=True)
            if first:
                new = jnp.maximum(top, NEGATIVE)
            else:
                old = top_ref[:, here]
                new = jnp.maximum(old, top)
                factor = jnp.exp2((old - new) * scale)
            exponents = jnp.exp2((scores - new) * scale).astype(jnp.bfloat16)
            added = jnp.dot(
                values_wide[:, : count * BLK], exponents, preferred_element_type=jnp.float32
            )
            if first:
                out[:, here] = added[:128]
                sum_ref[:, here] = added[128:129]
            else:
                out[:, here] = out[:, here] * factor + added[:128]
                sum_ref[:, here] = sum_ref[:, here] * factor + added[128:129]
            top_ref[:, here] = new
            return carry

        lax.fori_loop(0, heads * TILE // span, chunk, 0, unroll=8)

    values_wide[128:, :] = jnp.ones_like(values_wide[128:, :])

    def attend_picked(owner, group_of, first):
        wanted = picks(lambda entry: own_smem[0, 0, entry], owner, blocks, cap)
        values = [fill(slot, group_of[slot]) for slot in range(cap)]
        values_wide[:128, : cap * BLK] = jnp.concatenate(values, axis=0).T
        bounds = [
            jnp.where(wanted[slot] < 0, -FAR, first_pos - wanted[slot] * BLK) for slot in range(cap)
        ]
        attend(cap, bounds, 1, picked_top, picked_sum, picked_out, first)

    mine = picks(lambda entry: own_smem[0, 0, entry], me, blocks, cap)
    attend_picked(me, [packed[jnp.maximum(block - me * blocks, 0)] for block in mine], True)

    loads[5].wait()
    loads[6].wait()
    gates = jax.nn.sigmoid(
        lax.dot_general(
            gate_ref[...],
            hidden_ref[...],
            (((1,), (1,)), ((), ())),
            preferred_element_type=jnp.float32,
        )
    )

    def forward(step, carry):
        coarse_copy(step).wait_recv()
        pass_copy(step).start()
        return carry

    lax.fori_loop(1, n // 2, forward, 0)

    def passed(step, carry):
        pass_copy(step).wait_recv()
        return carry

    lax.fori_loop(0, n // 2, passed, 0)

    pieces = min(n, 8)

    def coarse_step(index, first):
        values = [fill(piece, coarse[index * pieces + piece]) for piece in range(pieces)]
        values_wide[:128, : pieces * BLK] = jnp.concatenate(values, axis=0).T
        start = first_pos - (CLEN - 1) - index * (pieces * BLK * CSTRIDE)
        bounds = [start - piece * (BLK * CSTRIDE) for piece in range(pieces)]
        attend(pieces, bounds, CSTRIDE, coarse_top, coarse_sum, coarse_out, first)

    coarse_step(0, True)
    if n > pieces:

        def coarse_more(index, carry):
            coarse_step(index, False)
            return carry

        lax.fori_loop(1, n // pieces, coarse_more, 0)

    def picked_step(step, carry):
        slot_copy(step).wait_recv()
        owner = flip(me, step, n)
        attend_picked(owner, [incoming[step, slot] for slot in range(cap)], False)
        return carry

    lax.fori_loop(1, n, picked_step, 0)

    for head in range(heads):
        here = slice(head * 128, (head + 1) * 128)
        of_coarse = gates[head : head + 1] / coarse_sum[:, here]
        of_picked = gates[heads + head : heads + head + 1] / picked_sum[:, here]
        mixed = coarse_out[:, here] * of_coarse + picked_out[:, here] * of_picked
        attended[:, here] = mixed.T.astype(jnp.bfloat16)

    def part_copy(step):
        return pltpu.make_async_remote_copy(
            src_ref=partial.at[step],
            dst_ref=arrived.at[step],
            send_sem=part_send.at[step],
            recv_sem=part_recv.at[step],
            device_id={"grp": flip(group, step, groups)},
            device_id_type=MESH,
        )

    for step in reversed(range(1, groups)):
        weight_copy(step).wait()
        partial[step] = jnp.dot(
            attended[...], weights[step], preferred_element_type=jnp.float32
        ).astype(jnp.bfloat16)
        part_copy(step).start()
    weight_copy(0).wait()
    own_part[...] = jnp.dot(attended[...], weights[0], preferred_element_type=jnp.float32)

    def sent(step, carry):
        table_copy(step).wait_send()
        slot_copy(step).wait_send()
        return carry

    lax.fori_loop(1, n, sent, 0)

    def sent_coarse(step, carry):
        coarse_copy(step).wait_send()
        pass_copy(step).wait_send()
        return carry

    lax.fori_loop(1, n // 2, sent_coarse, 0)
    pass_copy(0).wait_send()
    total = own_part[...]
    for step in range(1, groups):
        part_copy(step).wait_recv()
        total = total + arrived[step].astype(jnp.float32)
    out_ref[...] = total.astype(out_ref.dtype)
    for step in range(1, groups):
        part_copy(step).wait_send()


def shards(
    queries,
    key_cache,
    group_value_cache,
    coarse_keys,
    coarse_values,
    hidden,
    gate_weight,
    out_weight,
    selected,
):
    n = lax.axis_size("seq")
    groups = lax.axis_size("grp")
    ctx_dev = key_cache.shape[1]
    heads = queries.shape[1]
    width = queries.shape[2]
    vwidth = group_value_cache.shape[2]
    rows = TILE * heads
    blocks = ctx_dev // BLK
    cap = max(1, 2 * SEL // n)
    columns = out_weight.shape[1] // groups
    pieces = min(n, 8)
    wide = max(pieces, cap) * BLK

    vmem = pl.BlockSpec(memory_space=pltpu.VMEM)
    hbm = pl.BlockSpec(memory_space=pl.ANY)
    dma = pltpu.SemaphoreType.DMA
    bf16, f32 = jnp.bfloat16, jnp.float32
    inputs = (
        queries.transpose(1, 2, 0),
        key_cache[0].T,
        group_value_cache.reshape(blocks, BLK, vwidth),
        coarse_keys[0],
        coarse_values[0],
        hidden,
        gate_weight[0].T,
    )
    return pl.pallas_call(
        functools.partial(kernel, n, groups, cap, width**-0.5 * math.log2(math.e)),
        out_shape=jax.ShapeDtypeStruct((TILE, columns), bf16),
        in_specs=[pl.BlockSpec(memory_space=pltpu.SMEM), vmem] + [hbm] * (len(inputs) + 1),
        out_specs=vmem,
        scratch_shapes=[pltpu.VMEM(one.shape, bf16) for one in inputs]
        + [
            pltpu.VMEM((blocks, UNIT, 128), bf16),
            pltpu.VMEM((256, rows), bf16),
            pltpu.VMEM((n, 1, 1, SEL), jnp.int32),
            pltpu.SMEM((n, 1, 1, SEL), jnp.int32),
            pltpu.VMEM((n, cap, UNIT, 128), bf16),
            pltpu.VMEM((n, cap, UNIT, 128), bf16),
            pltpu.VMEM((n, UNIT, 128), bf16),
            pltpu.VMEM((wide, 256), bf16),
            pltpu.VMEM((144, wide), bf16),
            pltpu.VMEM((1, rows), f32),
            pltpu.VMEM((1, rows), f32),
            pltpu.VMEM((vwidth, rows), f32),
            pltpu.VMEM((1, rows), f32),
            pltpu.VMEM((1, rows), f32),
            pltpu.VMEM((vwidth, rows), f32),
            pltpu.VMEM((TILE, heads * vwidth), bf16),
            pltpu.VMEM((groups, heads * vwidth, columns), bf16),
            pltpu.VMEM((groups, TILE, columns), bf16),
            pltpu.VMEM((groups, TILE, columns), bf16),
            pltpu.VMEM((TILE, columns), f32),
            dma((len(inputs),)),
            dma((groups,)),
            dma,
            dma((n,)),
            dma((n,)),
            dma((n,)),
            dma((n,)),
            dma((n // 2,)),
            dma((n // 2,)),
            dma((n // 2,)),
            dma((n // 2,)),
            dma((groups,)),
            dma((groups,)),
        ],
        compiler_params=pltpu.CompilerParams(
            collective_id=0, has_side_effects=True, vmem_limit_bytes=60 * 1024 * 1024
        ),
    )(selected, selected, *inputs, out_weight)


def solution(mesh):
    return jax.shard_map(
        shards,
        mesh=mesh,
        in_specs=(
            P("seq", "grp", None),
            P("grp", "seq", None),
            P("grp", "seq", None),
            P("grp", "seq", None),
            P("grp", "seq", None),
            P("seq", None),
            P("grp", None, None),
            P("grp", None),
            P("grp", "seq", None),
        ),
        out_specs=P("seq", "grp"),
        check_vma=False,
    )
```
